256 devices in a mesh: row: 32 (over x_hi, z, core), off: 8 (over y, x_lo).
Axes of the slice: x: 4 (x_hi: 2, x_lo: 2; x = x_hi * 2 + x_lo), y: 4, z: 8, core: 2. Of those that a mesh axis runs over, the one named last changes fastest.
Arguments:
- vectors: float32 [64, 32768], P(None, 'row'), may hold values from -6 to 6
- tiles: float32 [32768, 16384], P('row', 'off'), may hold values from -0.03125 to 0.03125
- live: int32 [32, 16], P('row', 'off'), may hold values from 256 to 1024
- energies: float32 [32768], P('row'), may hold values from 0.25 to 5.25
- precond: float32 [32768], P('row'), may hold values from 0.03 to 0.3
Outputs:
- basis: float32 [64, 32768], P(None, 'row')
- ritz: float32 [64, 64], replicated
The draws below stay inside these ranges and needn't reach their ends.
All inputs are finite; a program needn't handle non-finite values.
Results may differ from the reference program's by a relative error of at most 0.00025.
Values sent between devices are 32-bit elements; how exact they have to be, the bound alone decides.
No kernel may reach another device: no remote copies, remote signals or barrier semaphores. Data moves between devices by JAX's collectives and lax.ppermute only.
A program may use at most 64 MiB of HBM per device.

```python
import math
import jax
import jax.numpy as jnp
from jax import lax

K = 64
G = 1024
ITERS = 2
NOFF = 16
NROWS = 32768


def draw_energies(key, part):
    group_ids = (jnp.arange(NROWS) // G).astype(jnp.float32)
    ladder = 1.0 + 2.0 * group_ids / (NROWS // G - 1)
    factor = jax.random.uniform(key, (NROWS,), jnp.float32, 0.5, 1.5)
    return ladder * factor


def draw_live(key, part):
    entries = NROWS // G * NOFF
    key_vals, key_spot = jax.random.split(jax.random.fold_in(key, 17))
    flat = jax.random.randint(key_vals, (entries,), G // 4, G + 1)
    spot_index = jax.random.randint(key_spot, (), 0, entries)
    flat = flat.at[spot_index].set(G)
    flat = flat.at[(spot_index + 1) % entries].set(G // 4)
    return flat.reshape(entries // NOFF, NOFF).astype(jnp.int32)


def block_levels(stream_key, dims, cuts, smallest, high):
    def one(position, blocks):
        heights = jax.random.uniform(jax.random.fold_in(jax.random.fold_in(stream_key, 6), position), (blocks,), jnp.float32, smallest / len(cuts), high / len(cuts))
        return jnp.repeat(jnp.exp(heights), dims[position] // blocks).reshape((-1,) + (1,) * (len(dims) - position - 1))

    factor_of = one(*cuts[0])
    for cut in cuts[1:]:
        factor_of = factor_of * one(*cut)
    return factor_of


def bell_draw(key, shape, deviation, bound, shards=(), held_as=jnp.bfloat16):
    result = deviation * jax.random.normal(key, shape, jnp.float32)
    if shards:
        result = result * block_levels(key, shape, shards, -0.22, 0.18)
    return jnp.clip(result, -bound, bound).astype(held_as)


def setup_inputs(seed: int = 0) -> dict:
    arg_keys = jax.random.split(jax.random.key(seed), 6)
    vectors = bell_draw(arg_keys[0], (K, NROWS), 1.0, 6.0, ((1, 32),), jnp.float32)
    tiles = bell_draw(arg_keys[1], (NROWS, NOFF * G), (2 * NOFF * G) ** -0.5, 0.03125, ((0, 32), (1, 8)), jnp.float32)
    live = draw_live(jax.random.fold_in(arg_keys[5], 71), 0)
    energies = draw_energies(jax.random.fold_in(arg_keys[5], 71), 0)
    precond = jnp.clip(jnp.exp(math.log(0.3) - 2.3025852 * jax.random.uniform(arg_keys[4], (NROWS,), jnp.float32) ** block_levels(arg_keys[4], (NROWS,), ((0, 32),), -0.2, 0.2)), 0.03, 0.3)
    return dict(vectors=vectors, tiles=tiles, live=live, energies=energies, precond=precond)


def apply_ham(vectors, tiles, live, energies):
    ngroups = NROWS // G
    split = vectors.reshape(K, ngroups, G)
    blocks = tiles.reshape(ngroups, G, NOFF, G)
    row_ids = jnp.arange(G, dtype=jnp.int32)
    direct = jnp.zeros_like(split)
    returned = jnp.zeros_like(split)
    for offset in range(NOFF):
        keep = (row_ids[None, :] < live[:, offset][:, None]).astype(jnp.float32)
        block = blocks[:, :, offset, :] * keep[:, :, None]
        shifted = jnp.roll(split, -offset, axis=1)
        direct = direct + jnp.einsum("igc,kic->kig", block, shifted, precision=lax.Precision.HIGHEST)
        back = jnp.einsum("igc,kig->kic", block, split, precision=lax.Precision.HIGHEST)
        returned = returned + jnp.roll(back, offset, axis=1)
    return energies * vectors + (direct + returned).reshape(K, NROWS)


def product(left, right):
    return jnp.dot(left, right, precision=lax.Precision.HIGHEST, preferred_element_type=jnp.float32)


def reference(vectors, tiles, live, energies, precond):
    identity = jnp.eye(K, dtype=jnp.float32)
    ritz_matrix = jnp.zeros((K, K), jnp.float32)
    for iteration in range(ITERS):
        image = apply_ham(vectors, tiles, live, energies)
        ritz_matrix = product(vectors, image.T) / NROWS
        resid = image - product(ritz_matrix.T, vectors)
        moved = vectors - precond * resid
        correlation = product(moved, moved.T) / NROWS
        vectors = product((1.5 * identity - 0.5 * correlation).T, moved)
    return vectors, ritz_matrix
```

```python
import jax
import jax.numpy as jnp
from jax import lax
from jax.sharding import PartitionSpec as P

ITERS = 2
AXES = ("row", "off")


class Layout:
    def __init__(self, rows, offs, per_device):
        self.rows, self.offs, self.per = rows, offs, per_device
        number = lambda row, off: (row % rows) * offs + off
        self.coupled = [[number(g - per_device * p, p) for p in range(offs)] for g in range(rows)]
        self.plane = [
            [number(2 * chip + core, p) for core in range(2) for p in range(offs)]
            for chip in range(rows // 2)
        ]
        self.line = [
            [number(2 * chip + core, p) for chip in range(rows // 2)]
            for core in range(2)
            for p in range(offs)
        ]
        self.swap = [
            (number(row, p), number(row ^ 1, p)) for row in range(rows) for p in range(offs)
        ]
        self.fetch = [
            [(number(row, p), number(row - per_device * p - s, p)) for row in range(rows) for p in range(offs)]
            for s in range(per_device)
        ]
        self.back = [[(b, a) for a, b in pairs] for pairs in self.fetch]


def exchange(array, groups):
    return lax.all_to_all(array, AXES, 0, 0, axis_index_groups=groups, tiled=True)


def sent_to_all(array, groups):
    peers = len(groups[0])
    return exchange(jnp.broadcast_to(array[None], (peers, *array.shape)), groups)


def exact(left, right):
    return jnp.dot(left, right, precision=lax.Precision.HIGHEST, preferred_element_type=jnp.float32)


def gram(left, right):
    return lax.dot_general(
        left,
        right,
        (((1,), (1,)), ((), ())),
        precision=lax.Precision.HIGHEST,
        preferred_element_type=jnp.float32,
    )


def cut(array, parts):
    k, width = array.shape
    return array.reshape(k, parts, width // parts).transpose(1, 0, 2)


def joined(array):
    parts, k, w = array.shape
    return array.transpose(1, 0, 2).reshape(k, parts * w)


def folded(square):
    half = square.shape[0] // 2
    return jnp.concatenate([square[:half], square[half:]], axis=1)


def unfolded(array):
    half = array.shape[0]
    return jnp.concatenate([array[:, : 2 * half], array[:, 2 * half :]], axis=0)


def summed_everywhere(square, lay):
    part = jnp.sum(sent_to_all(folded(square), lay.plane), axis=0)
    return unfolded(jnp.sum(sent_to_all(part, lay.line), axis=0))


def summed_over_rows(square, lay):
    part = jnp.sum(sent_to_all(folded(square), lay.line), axis=0)
    return unfolded(part + lax.ppermute(part, AXES, lay.swap))


def direct_product(piece, block, mask):
    term = lax.dot_general(
        piece,
        block,
        (((1,), (1,)), ((), ())),
        precision=lax.Precision.HIGH,
        preferred_element_type=jnp.float32,
    )
    return mask * term


def back_product(vectors, block, mask):
    return jnp.dot(
        vectors * mask, block, precision=lax.Precision.HIGH, preferred_element_type=jnp.float32
    )


def fetched(chunk, lay):
    near = jnp.stack([lax.ppermute(chunk, AXES, pairs) for pairs in lay.fetch])
    return sent_to_all(near, lay.coupled)


def returned(vectors, blocks, masks, lay):
    partials = jnp.stack(
        [cut(back_product(vectors, b, m), lay.offs) for b, m in zip(blocks, masks)], axis=1
    )
    near = jnp.sum(exchange(partials, lay.coupled), axis=0)
    return [lax.ppermute(near[s], AXES, pairs) for s, pairs in enumerate(lay.back)]


def directed(pieces, blocks, masks):
    total = None
    for piece, block, mask in zip(pieces, blocks, masks):
        term = direct_product(piece, block, mask)
        total = term if total is None else total + term
    return total


def local(vectors, tiles, live, energies, precond):
    count, width = vectors.shape
    per_device = tiles.shape[1] // width
    rows, offs = lax.axis_size("row"), lax.axis_size("off")
    lay = Layout(rows, offs, per_device)
    total_rows = width * rows
    part = width // offs
    off_index = lax.axis_index("off")
    row_ids = jnp.arange(width, dtype=jnp.int32)
    masks = [(row_ids < live[0, s]).astype(jnp.float32) for s in range(per_device)]
    blocks = [tiles[:, s * width : (s + 1) * width] for s in range(per_device)]
    identity = jnp.eye(count, dtype=jnp.float32)
    own = lambda array: lax.dynamic_index_in_dim(cut(array, offs), off_index, 0, keepdims=False)
    energy_chunk = own(energies[None])
    precond_chunk = own(precond[None])
    by_row = [[p for p in range(row * offs, (row + 1) * offs)] for row in range(rows)]

    def sweep(vecs, chunk, pieces):
        backs = returned(vecs, blocks, masks, lay)
        direct = directed(pieces(), blocks, masks)
        pair = gram(vecs, direct)
        diagonal = gram(vecs, energies * vecs) * (1.0 / offs)
        ritz = summed_everywhere(pair + pair.T + diagonal, lay) / total_rows
        summed = jnp.sum(exchange(cut(direct, offs), by_row), axis=0)
        image = energy_chunk * chunk + summed
        for b in backs:
            image = image + b
        return image, ritz

    chunk = own(vectors)
    packed = jnp.concatenate([chunk, jnp.broadcast_to(precond_chunk, (8, part))], axis=0)
    got = fetched(packed, lay)
    first_pieces = [joined(got[:, s, :count]) for s in range(per_device)]
    piece_precond = [joined(got[:, s, count : count + 1]) for s in range(per_device)]
    image, ritz = sweep(vectors, chunk, lambda: first_pieces)
    stepped = chunk - precond_chunk * image

    own_stepped = joined(sent_to_all(stepped, by_row))
    far = fetched(stepped, lay)
    moved = own_stepped + precond * exact(ritz.T, vectors)
    moved_chunk = own(moved)
    correlation = summed_over_rows(gram(moved, moved), lay) / total_rows
    fix = 1.5 * identity - 0.5 * correlation

    def second_pieces():
        return [
            joined(far[:, s]) + piece_precond[s] * exact(ritz.T, first_pieces[s])
            for s in range(per_device)
        ]

    image, ritz = sweep(moved, moved_chunk, second_pieces)
    image = exact(fix.T, image)
    ritz = exact(exact(fix.T, ritz), fix)
    chunk = exact(fix.T, moved_chunk)
    stepped = chunk - precond_chunk * image

    own_stepped = joined(sent_to_all(stepped, by_row))
    moved = own_stepped + precond * exact(ritz.T, exact(fix.T, moved))
    correlation = summed_over_rows(gram(moved, moved), lay) / total_rows
    return exact((1.5 * identity - 0.5 * correlation).T, moved), ritz


def solution(mesh):
    placed = (P(None, "row"), P("row", "off"), P("row", "off"), P("row"), P("row"))
    return jax.shard_map(
        local, mesh=mesh, in_specs=placed, out_specs=(P(None, "row"), P()), check_vma=False
    )
```

```python
import jax
import jax.numpy as jnp
from jax import lax
from jax.sharding import PartitionSpec as P

ITERS = 2
AXES = ("row", "off")


class Layout:
    def __init__(self, rows, offs, per_device):
        self.rows, self.offs, self.per = rows, offs, per_device
        number = lambda row, off: (row % rows) * offs + off
        every = [(row, p) for row in range(rows) for p in range(offs)]
        self.coupled = [[number(g - per_device * p, p) for p in range(offs)] for g in range(rows)]
        self.row = [[number(row, p) for p in range(offs)] for row in range(rows)]
        self.line = [
            [number(2 * chip + core, p) for chip in range(rows // 2)]
            for core in range(2)
            for p in range(offs)
        ]
        self.flip = {
            bit: [(number(row, p), number(row ^ bit, p)) for row, p in every]
            for bit in (1 << n for n in range(rows.bit_length() - 1))
        }
        self.back = [(number(row, p), number(row + per_device * p, p)) for row, p in every]
        self.fetch = [(b, a) for a, b in self.back]
        self.up = [(number(row, p), number(row + 1, p)) for row, p in every]
        self.down = [(b, a) for a, b in self.up]


def exchange(array, groups):
    return lax.all_to_all(array, AXES, 0, 0, axis_index_groups=groups, tiled=True)


def sent_to_all(array, groups):
    peers = len(groups[0])
    return exchange(jnp.broadcast_to(array[None], (peers, *array.shape)), groups)


def exact(left, right):
    return jnp.dot(left, right, precision=lax.Precision.HIGHEST, preferred_element_type=jnp.float32)


def gram(left, right):
    return lax.dot_general(
        left,
        right,
        (((1,), (1,)), ((), ())),
        precision=lax.Precision.HIGHEST,
        preferred_element_type=jnp.float32,
    )


def cut(array, parts):
    k, width = array.shape
    return array.reshape(k, parts, width // parts).transpose(1, 0, 2)


def joined(array):
    parts, k, w = array.shape
    return array.transpose(1, 0, 2).reshape(k, parts * w)


def folded(square):
    half = square.shape[0] // 2
    return jnp.concatenate([square[:half], square[half:]], axis=1)


def unfolded(array):
    half = array.shape[0]
    return jnp.concatenate([array[:, : 2 * half], array[:, 2 * half :]], axis=0)


def permuted(array, pairs):
    return lax.ppermute(array, AXES, pairs)


def row_total(part, lay):
    for pairs in lay.flip.values():
        part = part + permuted(part, pairs)
    return part


def row_total_late(part, lay):
    part = jnp.sum(sent_to_all(part, lay.line), axis=0)
    return part + permuted(part, lay.flip[1])


def direct_product(piece, block, mask):
    term = lax.dot_general(
        piece,
        block,
        (((1,), (1,)), ((), ())),
        precision=lax.Precision.HIGH,
        preferred_element_type=jnp.float32,
    )
    return mask * term


def back_product(vectors, block, mask):
    return jnp.dot(
        vectors * mask, block, precision=lax.Precision.HIGH, preferred_element_type=jnp.float32
    )


def local(vectors, tiles, live, energies, precond):
    count, width = vectors.shape
    per_device = tiles.shape[1] // width
    rows, offs = lax.axis_size("row"), lax.axis_size("off")
    lay = Layout(rows, offs, per_device)
    total_rows = width * rows
    part = width // offs
    off_index = lax.axis_index("off")
    row_ids = jnp.arange(width, dtype=jnp.int32)
    masks = [(row_ids < live[0, s]).astype(jnp.float32) for s in range(per_device)]
    blocks = [tiles[:, s * width : (s + 1) * width] for s in range(per_device)]
    identity = jnp.eye(count, dtype=jnp.float32)
    own = lambda array: lax.dynamic_index_in_dim(cut(array, offs), off_index, 0, keepdims=False)
    energy_chunk = own(energies[None])
    precond_chunk = own(precond[None])

    def back_products(vecs):
        far = permuted(back_product(vecs, blocks[1], masks[1]), lay.up)
        return cut(back_product(vecs, blocks[0], masks[0]) + far, offs)

    def direct_products(near, far):
        return direct_product(near, blocks[0], masks[0]) + direct_product(far, blocks[1], masks[1])

    def with_ritz(vecs, direct):
        pair = gram(vecs, direct)
        share = pair + pair.T + gram(vecs, energies * vecs) * (1.0 / offs)
        share = jnp.broadcast_to(folded(share)[None], (offs, count // 2, 2 * count))
        return jnp.concatenate([cut(direct, offs), share], axis=1)

    def collected(partial, direct):
        got = exchange(partial, lay.coupled)
        got, direct = lax.optimization_barrier((got, direct))
        back = permuted(jnp.sum(got, axis=0), lay.back)
        return back, jnp.sum(exchange(direct, lay.row), axis=0)

    chunk = own(vectors)
    packed = jnp.concatenate([chunk, jnp.broadcast_to(precond_chunk, (8, part))], axis=0)
    got = sent_to_all(permuted(packed, lay.fetch), lay.coupled)
    partial = back_products(vectors)
    partial, got = lax.optimization_barrier((partial, got))
    near = joined(got[:, :count])
    near_pre = joined(got[:, count:])
    far_both = permuted(jnp.concatenate([near, near_pre], axis=0), lay.down)
    far, far_pre = far_both[:count], far_both[count : count + 1]
    near_pre = near_pre[:1]
    back, summed = collected(partial, with_ritz(vectors, direct_products(near, far)))
    stepped = chunk - precond_chunk * (energy_chunk * chunk + summed[:count] + back)
    ritz = unfolded(row_total(summed[count:], lay)) / total_rows

    own_stepped = joined(sent_to_all(stepped, lay.row))
    near_stepped = joined(sent_to_all(permuted(stepped, lay.fetch), lay.coupled))
    far_stepped = permuted(near_stepped, lay.down)
    moved = own_stepped + precond * exact(ritz.T, vectors)
    near = near_stepped + near_pre * exact(ritz.T, near)
    far = far_stepped + far_pre * exact(ritz.T, far)
    moved_chunk = own(moved)
    correlation = unfolded(row_total(folded(gram(moved, moved)), lay)) / total_rows
    fix = 1.5 * identity - 0.5 * correlation
    back, summed = collected(back_products(moved), with_ritz(moved, direct_products(near, far)))
    image = exact(fix.T, energy_chunk * moved_chunk + summed[:count] + back)
    chunk = exact(fix.T, moved_chunk)
    stepped = chunk - precond_chunk * image
    ritz = unfolded(row_total(summed[count:], lay)) / total_rows
    ritz = exact(exact(fix.T, ritz), fix)

    own_stepped = joined(sent_to_all(stepped, lay.row))
    moved = own_stepped + precond * exact(ritz.T, exact(fix.T, moved))
    correlation = unfolded(row_total_late(folded(gram(moved, moved)), lay)) / total_rows
    return exact((1.5 * identity - 0.5 * correlation).T, moved), ritz


def solution(mesh):
    placed = (P(None, "row"), P("row", "off"), P("row", "off"), P("row"), P("row"))
    return jax.shard_map(
        local, mesh=mesh, in_specs=placed, out_specs=(P(None, "row"), P()), check_vma=False
    )
```

```python
import jax
import jax.numpy as jnp
from jax import lax
from jax.sharding import PartitionSpec as P

ITERS = 2
AXES = ("row", "off")


class Layout:
    def __init__(self, rows, offs, per_device):
        self.rows, self.offs, self.per = rows, offs, per_device
        number = lambda row, off: (row % rows) * offs + off
        every = [(row, p) for row in range(rows) for p in range(offs)]
        self.coupled = [[number(g - per_device * p, p) for p in range(offs)] for g in range(rows)]
        self.row = [[number(row, p) for p in range(offs)] for row in range(rows)]
        self.line = [
            [number(2 * chip + core, p) for chip in range(rows // 2)]
            for core in range(2)
            for p in range(offs)
        ]
        self.flip = {
            bit: [(number(row, p), number(row ^ bit, p)) for row, p in every]
            for bit in (1 << n for n in range(rows.bit_length() - 1))
        }
        self.fetch = [(number(row, p), number(row - per_device * p, p)) for row, p in every]
        self.back = [(b, a) for a, b in self.fetch]
        self.offs_flip = [[(number(row, p), number(row, p ^ d)) for row, p in every] for d in range(1, offs)]
        self.up = [(number(row, p), number(row + 1, p)) for row, p in every]
        self.down = [(b, a) for a, b in self.up]


def exchange(array, groups):
    return lax.all_to_all(array, AXES, 0, 0, axis_index_groups=groups, tiled=True)


def sent_to_all(array, groups):
    peers = len(groups[0])
    return exchange(jnp.broadcast_to(array[None], (peers, *array.shape)), groups)


def exact(left, right):
    return jnp.dot(left, right, precision=lax.Precision.HIGHEST, preferred_element_type=jnp.float32)


def gram(left, right):
    return lax.dot_general(
        left,
        right,
        (((1,), (1,)), ((), ())),
        precision=lax.Precision.HIGHEST,
        preferred_element_type=jnp.float32,
    )


def cut(array, parts):
    k, width = array.shape
    return array.reshape(k, parts, width // parts).transpose(1, 0, 2)


def joined(array):
    parts, k, w = array.shape
    return array.transpose(1, 0, 2).reshape(k, parts * w)


def folded(square):
    half = square.shape[0] // 2
    return jnp.concatenate([square[:half], square[half:]], axis=1)


def unfolded(array):
    half = array.shape[0]
    return jnp.concatenate([array[:, : 2 * half], array[:, 2 * half :]], axis=0)


def permuted(array, pairs):
    return lax.ppermute(array, AXES, pairs)


def window_total(part, lay):
    part = part + permuted(part, lay.flip[1])
    return part + permuted(part, lay.flip[lay.rows // 2])


def line_total(part, lay):
    part = jnp.sum(sent_to_all(part, lay.line), axis=0)
    return part + permuted(part, lay.flip[1])


def gathered(chunk, off_index, lay):
    pieces = jnp.stack([chunk] + [permuted(chunk, pairs) for pairs in lay.offs_flip])
    bits = lay.offs.bit_length() - 1
    pieces = pieces.reshape((2,) * bits + chunk.shape)
    for axis in range(bits):
        odd = off_index >> (bits - 1 - axis) & 1
        pieces = jnp.where(odd == 1, jnp.flip(pieces, axis), pieces)
    return joined(pieces.reshape((lay.offs,) + chunk.shape))


def direct_product(piece, block, mask):
    term = lax.dot_general(
        piece,
        block,
        (((1,), (1,)), ((), ())),
        precision=lax.Precision.HIGH,
        preferred_element_type=jnp.float32,
    )
    return mask * term


def back_product(vectors, block, mask):
    return jnp.dot(
        vectors * mask, block, precision=lax.Precision.HIGH, preferred_element_type=jnp.float32
    )


def local(vectors, tiles, live, energies, precond):
    count, width = vectors.shape
    per_device = tiles.shape[1] // width
    rows, offs = lax.axis_size("row"), lax.axis_size("off")
    lay = Layout(rows, offs, per_device)
    total_rows = width * rows
    part = width // offs
    off_index = lax.axis_index("off")
    row_ids = jnp.arange(width, dtype=jnp.int32)
    masks = [(row_ids < live[0, s]).astype(jnp.float32) for s in range(per_device)]
    blocks = [tiles[:, s * width : (s + 1) * width] for s in range(per_device)]
    identity = jnp.eye(count, dtype=jnp.float32)
    half = count // 2
    own = lambda array: lax.dynamic_index_in_dim(cut(array, offs), off_index, 0, keepdims=False)
    repeated = lambda square: jnp.broadcast_to(folded(square)[None], (offs, half, 2 * count))

    def back_products(vecs):
        far = permuted(back_product(vecs, blocks[1], masks[1]), lay.up)
        return cut(back_product(vecs, blocks[0], masks[0]) + far, offs)

    def direct_products(near, far):
        return direct_product(near, blocks[0], masks[0]) + direct_product(far, blocks[1], masks[1])

    def with_ritz(vecs, direct):
        pair = gram(vecs, direct)
        share = pair + pair.T + gram(vecs, energies * vecs) * (1.0 / offs)
        return jnp.concatenate([cut(direct, offs), repeated(share)], axis=1)

    def collected(partial, direct):
        got = jnp.sum(exchange(partial, lay.coupled), axis=0)
        got, direct = lax.optimization_barrier((got, direct))
        return got, jnp.sum(exchange(direct, lay.row), axis=0)

    packed = jnp.concatenate(
        [vectors, precond[None], energies[None], jnp.zeros((6, width), jnp.float32)], axis=0
    )
    packed_near = permuted(packed, lay.fetch)
    packed_far = permuted(packed_near, lay.down)
    near, far = packed_near[:count], packed_far[:count]
    precond_near, precond_far = packed_near[count : count + 1], packed_far[count : count + 1]
    chunk, precond_chunk, energy_chunk = own(vectors), own(precond[None]), own(energies[None])
    chunk_near, precond_chunk_near = own(near), own(precond_near)
    energy_chunk_near = own(packed_near[count + 1 : count + 2])
    back_near, summed = collected(back_products(vectors), with_ritz(vectors, direct_products(near, far)))
    back = permuted(back_near, lay.back)
    direct_near = permuted(summed[:count], lay.fetch)
    stepped = chunk - precond_chunk * (energy_chunk * chunk + (summed[:count] + back))
    stepped_near = chunk_near - precond_chunk_near * (
        energy_chunk_near * chunk_near + (direct_near + back_near)
    )

    got = sent_to_all(jnp.concatenate([stepped_near, summed[count:]], axis=0), lay.coupled)
    own_stepped = gathered(stepped, off_index, lay)
    near_stepped = joined(got[:, :count])
    far_stepped = permuted(near_stepped, lay.down)
    ritz = unfolded(window_total(jnp.sum(got[:, count:], axis=0), lay)) / total_rows
    moved = own_stepped + precond * exact(ritz.T, vectors)
    near = near_stepped + precond_near * exact(ritz.T, near)
    far = far_stepped + precond_far * exact(ritz.T, far)
    moved_chunk = own(moved)
    partial = jnp.concatenate([back_products(moved), repeated(gram(moved, moved))], axis=1)
    partial, near, far = lax.optimization_barrier((partial, near, far))
    back_near, summed = collected(partial, with_ritz(moved, direct_products(near, far)))
    back = permuted(back_near[:count], lay.back)
    correlation = unfolded(window_total(back_near[count:], lay)) / total_rows
    fix = 1.5 * identity - 0.5 * correlation
    image = exact(fix.T, energy_chunk * moved_chunk + (summed[:count] + back))
    chunk = exact(fix.T, moved_chunk)
    stepped = chunk - precond_chunk * image
    ritz = unfolded(line_total(summed[count:], lay)) / total_rows
    ritz = exact(exact(fix.T, ritz), fix)

    own_stepped = gathered(stepped, off_index, lay)
    moved = own_stepped + precond * exact(ritz.T, exact(fix.T, moved))
    correlation = unfolded(line_total(folded(gram(moved, moved)), lay)) / total_rows
    return exact((1.5 * identity - 0.5 * correlation).T, moved), ritz


def solution(mesh):
    placed = (P(None, "row"), P("row", "off"), P("row", "off"), P("row"), P("row"))
    return jax.shard_map(
        local, mesh=mesh, in_specs=placed, out_specs=(P(None, "row"), P()), check_vma=False
    )
```

```python
import jax
import jax.numpy as jnp
from jax import lax
from jax.sharding import PartitionSpec as P


AXES = ("row", "off")


class Layout:
    def __init__(self, rows, offs, per_device):
        self.rows, self.offs, self.per = rows, offs, per_device
        number = lambda row, off: (row % rows) * offs + off
        every = [(row, p) for row in range(rows) for p in range(offs)]
        self.row = [[number(row, p) for p in range(offs)] for row in range(rows)]
        self.line = [
            [number(2 * chip + core, p) for chip in range(rows // 2)]
            for core in range(2)
            for p in range(offs)
        ]
        self.flip = {
            bit: [(number(row, p), number(row ^ bit, p)) for row, p in every]
            for bit in (1 << n for n in range(rows.bit_length() - 1))
        }
        self.fetch = [(number(row, p), number(row - per_device * p, p)) for row, p in every]
        self.back = [(b, a) for a, b in self.fetch]
        self.up = [(number(row, p), number(row + 1, p)) for row, p in every]
        self.down = [(b, a) for a, b in self.up]


def exchange(array, groups):
    return lax.all_to_all(array, AXES, 0, 0, axis_index_groups=groups, tiled=True)


def sent_to_all(array, groups):
    peers = len(groups[0])
    return exchange(jnp.broadcast_to(array[None], (peers, *array.shape)), groups)


def exact(left, right):
    return jnp.dot(left, right, precision=lax.Precision.HIGHEST, preferred_element_type=jnp.float32)


def gram(left, right):
    return lax.dot_general(
        left,
        right,
        (((1,), (1,)), ((), ())),
        precision=lax.Precision.HIGHEST,
        preferred_element_type=jnp.float32,
    )


def cut(array, parts):
    k, width = array.shape
    return array.reshape(k, parts, width // parts).transpose(1, 0, 2)


def joined(array):
    parts, k, w = array.shape
    return array.transpose(1, 0, 2).reshape(k, parts * w)


def folded(square):
    half = square.shape[0] // 2
    return jnp.concatenate([square[:half], square[half:]], axis=1)


def unfolded(array):
    half = array.shape[0]
    return jnp.concatenate([array[:, : 2 * half], array[:, 2 * half :]], axis=0)


def permuted(array, pairs):
    return lax.ppermute(array, AXES, pairs)


def row_total(part, lay):
    for pairs in lay.flip.values():
        part = part + permuted(part, pairs)
    return part


def line_total(part, lay):
    part = jnp.sum(sent_to_all(part, lay.line), axis=0)
    return part + permuted(part, lay.flip[1])


def direct_product(piece, block, mask):
    term = lax.dot_general(
        piece,
        block,
        (((1,), (1,)), ((), ())),
        precision=lax.Precision.HIGH,
        preferred_element_type=jnp.float32,
    )
    return mask * term


def back_product(vectors, block, mask):
    return jnp.dot(
        vectors * mask, block, precision=lax.Precision.HIGH, preferred_element_type=jnp.float32
    )


def local(vectors, tiles, live, energies, precond):
    count, width = vectors.shape
    per_device = tiles.shape[1] // width
    rows, offs = lax.axis_size("row"), lax.axis_size("off")
    lay = Layout(rows, offs, per_device)
    total_rows = width * rows
    part = width // offs
    off_index = lax.axis_index("off")
    row_ids = jnp.arange(width, dtype=jnp.int32)
    masks = [(row_ids < live[0, s]).astype(jnp.float32) for s in range(per_device)]
    blocks = [tiles[:, s * width : (s + 1) * width] for s in range(per_device)]
    identity = jnp.eye(count, dtype=jnp.float32)
    own = lambda array: lax.dynamic_index_in_dim(cut(array, offs), off_index, 0, keepdims=False)

    def products(vecs, extra):
        near = permuted(vecs, lay.fetch)
        up = permuted(back_product(vecs, blocks[1], masks[1]), lay.up)
        back = lax.optimization_barrier(back_product(vecs, blocks[0], masks[0])) + up
        returned = permuted(back, lay.back)
        far = permuted(near, lay.down)
        pair = gram(near, back)
        share = folded(pair + pair.T + gram(vecs, energies * vecs) * (1.0 / offs))
        share = row_total(jnp.concatenate([share] + extra, axis=0), lay)
        direct = direct_product(near, blocks[0], masks[0]) + direct_product(far, blocks[1], masks[1])
        return lax.optimization_barrier(direct) + returned, share

    def spread(chunk, share):
        got = sent_to_all(jnp.concatenate([chunk, share], axis=0), lay.row)
        return joined(got[:, :count]), unfolded(jnp.sum(got[:, count:], axis=0)) / total_rows

    chunk, precond_chunk, energy_chunk = own(vectors), own(precond[None]), own(energies[None])
    part, share = products(vectors, [])
    image = energy_chunk * chunk + jnp.sum(exchange(cut(part, offs), lay.row), axis=0)
    stepped, ritz = spread(chunk - precond_chunk * image, share)
    moved = stepped + precond * exact(ritz.T, vectors)

    moved_chunk = own(moved)
    part, share = products(moved, [folded(gram(moved, moved))])
    image = energy_chunk * moved_chunk + jnp.sum(exchange(cut(part, offs), lay.row), axis=0)
    fix = 1.5 * identity - 0.5 * unfolded(share[count // 2 :]) / total_rows
    chunk = exact(fix.T, moved_chunk - precond_chunk * image)
    stepped, ritz = spread(chunk, share[: count // 2])
    ritz = exact(exact(fix.T, ritz), fix)
    moved = stepped + precond * exact(ritz.T, exact(fix.T, moved))

    correlation = unfolded(line_total(folded(gram(moved, moved)), lay)) / total_rows
    return exact((1.5 * identity - 0.5 * correlation).T, moved), ritz


def solution(mesh):
    placed = (P(None, "row"), P("row", "off"), P("row", "off"), P("row"), P("row"))
    return jax.shard_map(
        local, mesh=mesh, in_specs=placed, out_specs=(P(None, "row"), P()), check_vma=False
    )
```

```python
import jax
import jax.numpy as jnp
from jax import lax
from jax.sharding import PartitionSpec as P


AXES = ("row", "off")


class Layout:
    def __init__(self, rows, offs, per_device):
        self.rows, self.offs, self.per = rows, offs, per_device
        number = lambda row, off: (row % rows) * offs + off
        every = [(row, p) for row in range(rows) for p in range(offs)]
        self.row = [[number(row, p) for p in range(offs)] for row in range(rows)]
        self.line = [
            [number(2 * chip + core, p) for chip in range(rows // 2)]
            for core in range(2)
            for p in range(offs)
        ]
        self.flip = {
            bit: [(number(row, p), number(row ^ bit, p)) for row, p in every]
            for bit in (1 << n for n in range(rows.bit_length() - 1))
        }
        turn = lambda row: row // 2 * 2 % offs
        self.fetch = [
            (number(row, p ^ turn(row)), number(row - per_device * p, p)) for row, p in every
        ]
        self.back = [(b, a) for a, b in self.fetch]
        self.up = [(number(row, p), number(row + 1, p)) for row, p in every]
        self.down = [(b, a) for a, b in self.up]


def exchange(array, groups):
    return lax.all_to_all(array, AXES, 0, 0, axis_index_groups=groups, tiled=True)


def sent_to_all(array, groups):
    peers = len(groups[0])
    return exchange(jnp.broadcast_to(array[None], (peers, *array.shape)), groups)


def exact(left, right):
    return jnp.dot(left, right, precision=lax.Precision.HIGHEST, preferred_element_type=jnp.float32)


def gram(left, right):
    return lax.dot_general(
        left,
        right,
        (((1,), (1,)), ((), ())),
        precision=lax.Precision.HIGHEST,
        preferred_element_type=jnp.float32,
    )


def cut(array, parts):
    k, width = array.shape
    return array.reshape(k, parts, width // parts).transpose(1, 0, 2)


def joined(array):
    parts, k, w = array.shape
    return array.transpose(1, 0, 2).reshape(k, parts * w)


def folded(square):
    half = square.shape[0] // 2
    return jnp.concatenate([square[:half], square[half:]], axis=1)


def unfolded(array):
    half = array.shape[0]
    return jnp.concatenate([array[:, : 2 * half], array[:, 2 * half :]], axis=0)


def permuted(array, pairs):
    return lax.ppermute(array, AXES, pairs)


def row_total(part, lay):
    far = lay.rows // 2
    for bit in [1, far] + [bit for bit in lay.flip if bit not in (1, far)]:
        part = part + permuted(part, lay.flip[bit])
    return part


def line_total(part, lay):
    part = jnp.sum(sent_to_all(part, lay.line), axis=0)
    return part + permuted(part, lay.flip[1])


def direct_product(piece, block, mask):
    term = lax.dot_general(
        piece,
        block,
        (((1,), (1,)), ((), ())),
        precision=lax.Precision.HIGH,
        preferred_element_type=jnp.float32,
    )
    return mask * term


def back_product(vectors, block, mask):
    return jnp.dot(
        vectors * mask, block, precision=lax.Precision.HIGH, preferred_element_type=jnp.float32
    )


def local(vectors, tiles, live, energies, precond):
    count, width = vectors.shape
    per_device = tiles.shape[1] // width
    rows, offs = lax.axis_size("row"), lax.axis_size("off")
    lay = Layout(rows, offs, per_device)
    total_rows = width * rows
    part = width // offs
    off_index = lax.axis_index("off")
    row_ids = jnp.arange(width, dtype=jnp.int32)
    masks = [(row_ids < live[0, s]).astype(jnp.float32) for s in range(per_device)]
    blocks = [tiles[:, s * width : (s + 1) * width] for s in range(per_device)]
    identity = jnp.eye(count, dtype=jnp.float32)
    own = lambda array: lax.dynamic_index_in_dim(cut(array, offs), off_index, 0, keepdims=False)

    def products(vecs, extra):
        near = permuted(vecs, lay.fetch)
        up = permuted(back_product(vecs, blocks[1], masks[1]), lay.up)
        back = back_product(vecs, blocks[0], masks[0])
        back = lax.optimization_barrier(back) + up
        returned = permuted(back, lay.back)
        far = permuted(near, lay.down)
        pair = gram(near, back)
        share = folded(pair + pair.T + gram(vecs, energies * vecs) * (1.0 / offs))
        first = direct_product(near, blocks[0], masks[0])
        second = direct_product(far, blocks[1], masks[1])
        first, second = lax.optimization_barrier(first), lax.optimization_barrier(second)
        share = row_total(jnp.concatenate([share] + extra, axis=0), lay)
        return first + second + returned, share

    def spread(chunk, share):
        got = sent_to_all(jnp.concatenate([chunk, share], axis=0), lay.row)
        return joined(got[:, :count]), unfolded(jnp.sum(got[:, count:], axis=0)) / total_rows

    chunk, precond_chunk, energy_chunk = own(vectors), own(precond[None]), own(energies[None])
    part, share = products(vectors, [])
    image = energy_chunk * chunk + jnp.sum(exchange(cut(part, offs), lay.row), axis=0)
    stepped, ritz = spread(chunk - precond_chunk * image, share)
    moved = stepped + precond * exact(ritz.T, vectors)

    moved_chunk = own(moved)
    part, share = products(moved, [folded(gram(moved, moved))])
    image = energy_chunk * moved_chunk + jnp.sum(exchange(cut(part, offs), lay.row), axis=0)
    fix = 1.5 * identity - 0.5 * unfolded(share[count // 2 :]) / total_rows
    chunk = exact(fix.T, moved_chunk - precond_chunk * image)
    stepped, ritz = spread(chunk, share[: count // 2])
    ritz = exact(exact(fix.T, ritz), fix)
    moved = stepped + precond * exact(ritz.T, exact(fix.T, moved))

    correlation = unfolded(line_total(folded(gram(moved, moved)), lay)) / total_rows
    return exact((1.5 * identity - 0.5 * correlation).T, moved), ritz


def solution(mesh):
    placed = (P(None, "row"), P("row", "off"), P("row", "off"), P("row"), P("row"))
    return jax.shard_map(
        local, mesh=mesh, in_specs=placed, out_specs=(P(None, "row"), P()), check_vma=False
    )
```

```python
import jax
import jax.numpy as jnp
from jax import lax
from jax.sharding import PartitionSpec as P


AXES = ("row", "off")


class Layout:
    def __init__(self, rows, offs, per_device):
        self.rows, self.offs, self.per = rows, offs, per_device
        number = lambda row, off: (row % rows) * offs + off
        every = [(row, p) for row in range(rows) for p in range(offs)]
        self.row = [[number(row, p) for p in range(offs)] for row in range(rows)]
        self.line = [
            [number(2 * chip + core, p) for chip in range(rows // 2)]
            for core in range(2)
            for p in range(offs)
        ]
        self.flip = {
            bit: [(number(row, p), number(row ^ bit, p)) for row, p in every]
            for bit in (1 << n for n in range(rows.bit_length() - 1))
        }
        turn = lambda row: row // 2 * 2 % offs
        self.fetch = [
            (number(row, p ^ turn(row)), number(row - per_device * p, p)) for row, p in every
        ]
        self.back = [(b, a) for a, b in self.fetch]
        self.up = [(number(row, p), number(row + 1, p)) for row, p in every]
        self.down = [(b, a) for a, b in self.up]


def exchange(array, groups):
    return lax.all_to_all(array, AXES, 0, 0, axis_index_groups=groups, tiled=True)


def sent_to_all(array, groups):
    peers = len(groups[0])
    return exchange(jnp.broadcast_to(array[None], (peers, *array.shape)), groups)


def exact(left, right):
    return jnp.dot(left, right, precision=lax.Precision.HIGHEST, preferred_element_type=jnp.float32)


def gram(left, right):
    return lax.dot_general(
        left,
        right,
        (((1,), (1,)), ((), ())),
        precision=lax.Precision.HIGHEST,
        preferred_element_type=jnp.float32,
    )


def cut(array, parts):
    k, width = array.shape
    return array.reshape(k, parts, width // parts).transpose(1, 0, 2)


def joined(array):
    parts, k, w = array.shape
    return array.transpose(1, 0, 2).reshape(k, parts * w)


def folded(square):
    half = square.shape[0] // 2
    return jnp.concatenate([square[:half], square[half:]], axis=1)


def unfolded(array):
    half = array.shape[0]
    return jnp.concatenate([array[:, : 2 * half], array[:, 2 * half :]], axis=0)


def permuted(array, pairs):
    return lax.ppermute(array, AXES, pairs)


def row_total(part, lay):
    far = lay.rows // 2
    for bit in [1, far] + [bit for bit in lay.flip if bit not in (1, far)]:
        part = part + permuted(part, lay.flip[bit])
    return part


def line_total(part, lay):
    part = jnp.sum(sent_to_all(part, lay.line), axis=0)
    return part + permuted(part, lay.flip[1])


def halves(array):
    high = lax.reduce_precision(array, 8, 7)
    return high.astype(jnp.bfloat16), (array - high).astype(jnp.bfloat16)


def block_product(vecs, block, dims):
    high, low = halves(vecs)
    count = vecs.shape[0]
    dot = lambda left, right: lax.dot_general(
        left, right, (dims, ((), ())), preferred_element_type=jnp.float32
    )
    main = dot(jnp.concatenate([high, low], axis=0), block[0])
    return main[:count] + (main[count:] + dot(high, block[1]))


def direct_product(piece, block):
    return block_product(piece, block, ((1,), (1,)))


def back_product(vecs, block):
    return block_product(vecs, block, ((1,), (0,)))


def local(vectors, tiles, live, energies, precond):
    count, width = vectors.shape
    per_device = tiles.shape[1] // width
    rows, offs = lax.axis_size("row"), lax.axis_size("off")
    lay = Layout(rows, offs, per_device)
    total_rows = width * rows
    part = width // offs
    off_index = lax.axis_index("off")
    row_ids = jnp.arange(width, dtype=jnp.int32)[:, None]
    block_of = lambda array, s: array[:, s * width : (s + 1) * width]

    def split_of(array, s):
        return lax.optimization_barrier(
            halves(jnp.where(row_ids < live[0, s], block_of(array, s), 0.0))
        )

    masks = [(row_ids[:, 0] < live[0, s]).astype(jnp.float32) for s in range(per_device)]

    def back_first(vecs, s):
        return jnp.dot(
            vecs * masks[s],
            block_of(tiles, s),
            precision=lax.Precision.HIGH,
            preferred_element_type=jnp.float32,
        )

    def direct_first(piece, s):
        return masks[s] * lax.dot_general(
            piece,
            block_of(tiles, s),
            (((1,), (1,)), ((), ())),
            precision=lax.Precision.HIGH,
            preferred_element_type=jnp.float32,
        )

    identity = jnp.eye(count, dtype=jnp.float32)
    own = lambda array: lax.dynamic_index_in_dim(cut(array, offs), off_index, 0, keepdims=False)

    def products(vecs, extra, back_of, direct_of):
        near = permuted(vecs, lay.fetch)
        up = permuted(back_of(vecs, 1), lay.up)
        back = lax.optimization_barrier(back_of(vecs, 0))
        back = back + up
        returned = permuted(back, lay.back)
        far = permuted(near, lay.down)
        pair = gram(near, back)
        share = folded(pair + pair.T + gram(vecs, energies * vecs) * (1.0 / offs))
        first = lax.optimization_barrier(direct_of(near, 0))
        second = lax.optimization_barrier(direct_of(far, 1))
        share = row_total(jnp.concatenate([share] + extra, axis=0), lay)
        return first + second + returned, share

    def spread(chunk, share):
        got = sent_to_all(jnp.concatenate([chunk, share], axis=0), lay.row)
        return joined(got[:, :count]), unfolded(jnp.sum(got[:, count:], axis=0)) / total_rows

    chunk, precond_chunk, energy_chunk = own(vectors), own(precond[None]), own(energies[None])
    part, share = products(vectors, [], back_first, direct_first)
    part, later = lax.optimization_barrier((part, tiles))
    blocks = []
    for s in range(per_device):
        blocks.append(split_of(later, s))
        blocks[-1], later = lax.optimization_barrier((blocks[-1], later))
    image = jnp.sum(exchange(cut(part, offs), lay.row), axis=0)
    image = energy_chunk * chunk + image
    stepped, ritz = spread(chunk - precond_chunk * image, share)
    moved = stepped + precond * exact(ritz.T, vectors)

    moved_chunk = own(moved)
    part, share = products(
        moved,
        [folded(gram(moved, moved))],
        lambda vecs, s: back_product(vecs, blocks[s]),
        lambda piece, s: direct_product(piece, blocks[s]),
    )
    image = energy_chunk * moved_chunk + jnp.sum(exchange(cut(part, offs), lay.row), axis=0)
    fix = 1.5 * identity - 0.5 * unfolded(share[count // 2 :]) / total_rows
    chunk = exact(fix.T, moved_chunk - precond_chunk * image)
    stepped, ritz = spread(chunk, share[: count // 2])
    ritz = exact(exact(fix.T, ritz), fix)
    moved = stepped + precond * exact(ritz.T, exact(fix.T, moved))

    correlation = unfolded(line_total(folded(gram(moved, moved)), lay)) / total_rows
    return exact((1.5 * identity - 0.5 * correlation).T, moved), ritz


def solution(mesh):
    placed = (P(None, "row"), P("row", "off"), P("row", "off"), P("row"), P("row"))
    return jax.shard_map(
        local, mesh=mesh, in_specs=placed, out_specs=(P(None, "row"), P()), check_vma=False
    )
```

```python
import jax
import jax.numpy as jnp
from jax import lax
from jax.sharding import PartitionSpec as P


AXES = ("row", "off")


class Layout:
    def __init__(self, rows, offs, per_device):
        self.rows, self.offs, self.per = rows, offs, per_device
        number = lambda row, off: (row % rows) * offs + off
        every = [(row, p) for row in range(rows) for p in range(offs)]
        self.row = [[number(row, p) for p in range(offs)] for row in range(rows)]
        self.line = [
            [number(2 * chip + core, p) for chip in range(rows // 2)]
            for core in range(2)
            for p in range(offs)
        ]
        self.flip = {
            bit: [(number(row, p), number(row ^ bit, p)) for row, p in every]
            for bit in (1 << n for n in range(rows.bit_length() - 1))
        }
        turn = lambda row: row % rows // 2 * 2 % offs

        def couple(row, p, s):
            far = row + per_device * p + s
            return number(far, p ^ turn(far)), number(row, p)

        self.fetch = [couple(row, p, 0) for row, p in every]
        self.back = [(b, a) for a, b in self.fetch]
        self.fetch_odd = [couple(row, p, 1) for row, p in every if row % 2]
        self.back_odd = [(b, a) for a, b in self.fetch_odd]
        self.to_odd = [(number(row - 1, p), number(row, p)) for row, p in every if row % 2]
        self.to_even = [(b, a) for a, b in self.to_odd]


def exchange(array, groups):
    return lax.all_to_all(array, AXES, 0, 0, axis_index_groups=groups, tiled=True)


def sent_to_all(array, groups):
    peers = len(groups[0])
    return exchange(jnp.broadcast_to(array[None], (peers, *array.shape)), groups)


def exact(left, right):
    return jnp.dot(left, right, precision=lax.Precision.HIGHEST, preferred_element_type=jnp.float32)


def gram(left, right):
    return lax.dot_general(
        left,
        right,
        (((1,), (1,)), ((), ())),
        precision=lax.Precision.HIGHEST,
        preferred_element_type=jnp.float32,
    )


def cut(array, parts):
    k, width = array.shape
    return array.reshape(k, parts, width // parts).transpose(1, 0, 2)


def joined(array):
    parts, k, w = array.shape
    return array.transpose(1, 0, 2).reshape(k, parts * w)


def folded(square):
    half = square.shape[0] // 2
    return jnp.concatenate([square[:half], square[half:]], axis=1)


def unfolded(array):
    half = array.shape[0]
    return jnp.concatenate([array[:, : 2 * half], array[:, 2 * half :]], axis=0)


def permuted(array, pairs):
    return lax.ppermute(array, AXES, pairs)


def row_total(part, lay):
    far = lay.rows // 2
    for bit in [1, far] + [bit for bit in lay.flip if bit not in (1, far)]:
        part = part + permuted(part, lay.flip[bit])
    return part


def line_total(part, lay):
    part = jnp.sum(sent_to_all(part, lay.line), axis=0)
    return part + permuted(part, lay.flip[1])


def halves(array):
    high = lax.reduce_precision(array, 8, 7)
    return high.astype(jnp.bfloat16), (array - high).astype(jnp.bfloat16)


def block_product(vecs, block, dims):
    high, low = halves(vecs)
    count = vecs.shape[0]
    dot = lambda left, right: lax.dot_general(
        left, right, (dims, ((), ())), preferred_element_type=jnp.float32
    )
    main = dot(jnp.concatenate([high, low], axis=0), block[0])
    return main[:count] + (main[count:] + dot(high, block[1]))


def direct_product(piece, block):
    return block_product(piece, block, ((1,), (1,)))


def back_product(vecs, block):
    return block_product(vecs, block, ((1,), (0,)))


def local(vectors, tiles, live, energies, precond):
    count, width = vectors.shape
    per_device = tiles.shape[1] // width
    rows, offs = lax.axis_size("row"), lax.axis_size("off")
    lay = Layout(rows, offs, per_device)
    total_rows = width * rows
    part = width // offs
    off_index = lax.axis_index("off")
    odd = (lax.axis_index("row") % 2).astype(jnp.float32)
    row_ids = jnp.arange(width, dtype=jnp.int32)[:, None]
    block_of = lambda array, s: array[:, s * width : (s + 1) * width]

    def split_of(array, s):
        return lax.optimization_barrier(
            halves(jnp.where(row_ids < live[0, s], block_of(array, s), 0.0))
        )

    masks = (lax.broadcasted_iota(jnp.int32, (per_device, width), 1) < live.T).astype(jnp.float32)
    masks = lax.optimization_barrier(masks)

    def back_first(vecs, s):
        return jnp.dot(
            vecs * masks[s],
            block_of(tiles, s),
            precision=lax.Precision.HIGH,
            preferred_element_type=jnp.float32,
        )

    identity = jnp.eye(count, dtype=jnp.float32)
    own = lambda array: lax.dynamic_index_in_dim(cut(array, offs), off_index, 0, keepdims=False)

    def products(vecs, extra, back_of, block_for):
        near = permuted(vecs, lay.fetch)
        far = permuted(vecs, lay.fetch_odd)
        back_far = lax.optimization_barrier(back_of(vecs, 1))
        up = permuted(back_far, lay.to_odd)
        returned_far = permuted(back_far, lay.back_odd)
        own_back = lax.optimization_barrier(back_of(vecs, 0))
        back = own_back + up
        returned = permuted(back, lay.back)
        far = far + permuted(near, lay.to_even)
        pair = gram(near, back) + gram(far, back_far * odd)
        share = folded(pair + pair.T + gram(vecs, energies * vecs) * (1.0 / offs))
        block = block_for(0, own_back)
        first = lax.optimization_barrier(direct_product(near, block))
        block = block_for(1, block)
        second = lax.optimization_barrier(direct_product(far, block))
        share = row_total(jnp.concatenate([share] + extra, axis=0), lay)
        return first + second + (returned + returned_far), share

    def spread(chunk, share):
        got = sent_to_all(jnp.concatenate([chunk, share], axis=0), lay.row)
        return joined(got[:, :count]), unfolded(jnp.sum(got[:, count:], axis=0)) / total_rows

    chunk, precond_chunk, energy_chunk = own(vectors), own(precond[None]), own(energies[None])
    blocks = []

    def split_after(s, earlier):
        blocks.append(split_of(lax.optimization_barrier((tiles, earlier))[0], s))
        return blocks[s]

    part, share = products(vectors, [], back_first, split_after)
    image = jnp.sum(exchange(cut(part, offs), lay.row), axis=0)
    image = energy_chunk * chunk + image
    stepped, ritz = spread(chunk - precond_chunk * image, share)
    moved = stepped + precond * exact(ritz.T, vectors)

    moved_chunk = own(moved)
    part, share = products(
        moved,
        [folded(gram(moved, moved))],
        lambda vecs, s: back_product(vecs, blocks[s]),
        lambda s, _: blocks[s],
    )
    image = energy_chunk * moved_chunk + jnp.sum(exchange(cut(part, offs), lay.row), axis=0)
    fix = 1.5 * identity - 0.5 * unfolded(share[count // 2 :]) / total_rows
    chunk = exact(fix.T, moved_chunk - precond_chunk * image)
    stepped, ritz = spread(chunk, share[: count // 2])
    ritz = exact(exact(fix.T, ritz), fix)
    moved = stepped + precond * exact(ritz.T, exact(fix.T, moved))

    correlation = unfolded(line_total(folded(gram(moved, moved)), lay)) / total_rows
    return exact((1.5 * identity - 0.5 * correlation).T, moved), ritz


def solution(mesh):
    placed = (P(None, "row"), P("row", "off"), P("row", "off"), P("row"), P("row"))
    return jax.shard_map(
        local, mesh=mesh, in_specs=placed, out_specs=(P(None, "row"), P()), check_vma=False
    )
```

```python
import jax
import jax.numpy as jnp
from jax import lax
from jax.sharding import PartitionSpec as P


AXES = ("row", "off")


class Layout:
    def __init__(self, rows, offs, per_device):
        self.rows, self.offs, self.per = rows, offs, per_device
        number = lambda row, off: (row % rows) * offs + off
        every = [(row, p) for row in range(rows) for p in range(offs)]
        self.row = [[number(row, p) for p in range(offs)] for row in range(rows)]
        self.line = [
            [number(2 * chip + core, p) for chip in range(rows // 2)]
            for core in range(2)
            for p in range(offs)
        ]
        self.flip = {
            bit: [(number(row, p), number(row ^ bit, p)) for row, p in every]
            for bit in (1 << n for n in range(rows.bit_length() - 1))
        }
        turn = lambda row: row // 2 * 2 % offs
        self.fetch = [
            (number(row, p ^ turn(row)), number(row - per_device * p, p)) for row, p in every
        ]
        self.back = [(b, a) for a, b in self.fetch]
        self.up = [(number(row, p), number(row + 1, p)) for row, p in every]
        self.down = [(b, a) for a, b in self.up]


def exchange(array, groups):
    return lax.all_to_all(array, AXES, 0, 0, axis_index_groups=groups, tiled=True)


def sent_to_all(array, groups):
    peers = len(groups[0])
    return exchange(jnp.broadcast_to(array[None], (peers, *array.shape)), groups)


def exact(left, right):
    return jnp.dot(left, right, precision=lax.Precision.HIGHEST, preferred_element_type=jnp.float32)


def gram(left, right):
    return lax.dot_general(
        left,
        right,
        (((1,), (1,)), ((), ())),
        precision=lax.Precision.HIGHEST,
        preferred_element_type=jnp.float32,
    )


def cut(array, parts):
    k, width = array.shape
    return array.reshape(k, parts, width // parts).transpose(1, 0, 2)


def joined(array):
    parts, k, w = array.shape
    return array.transpose(1, 0, 2).reshape(k, parts * w)


def folded(square):
    half = square.shape[0] // 2
    return jnp.concatenate([square[:half], square[half:]], axis=1)


def unfolded(array):
    half = array.shape[0]
    return jnp.concatenate([array[:, : 2 * half], array[:, 2 * half :]], axis=0)


def permuted(array, pairs):
    return lax.ppermute(array, AXES, pairs)


def row_total(part, lay):
    for bit in sorted(lay.flip, reverse=True):
        part = part + permuted(part, lay.flip[bit])
    return part


def line_total(part, lay):
    part = jnp.sum(sent_to_all(part, lay.line), axis=0)
    return part + permuted(part, lay.flip[1])


def halves(array):
    high = lax.reduce_precision(array, 8, 7)
    return high.astype(jnp.bfloat16), (array - high).astype(jnp.bfloat16)


def block_product(vecs, block, dims):
    high, low = halves(vecs)
    count = vecs.shape[0]
    dot = lambda left, right: lax.dot_general(
        left, right, (dims, ((), ())), preferred_element_type=jnp.float32
    )
    main = dot(jnp.concatenate([high, low], axis=0), block[0])
    return main[:count] + (main[count:] + dot(high, block[1]))


def direct_product(piece, block):
    return block_product(piece, block, ((1,), (1,)))


def back_product(vecs, block):
    return block_product(vecs, block, ((1,), (0,)))


def local(vectors, tiles, live, energies, precond):
    count, width = vectors.shape
    per_device = tiles.shape[1] // width
    rows, offs = lax.axis_size("row"), lax.axis_size("off")
    lay = Layout(rows, offs, per_device)
    total_rows = width * rows
    part = width // offs
    off_index = lax.axis_index("off")
    row_ids = jnp.arange(width, dtype=jnp.int32)[:, None]
    block_of = lambda array, s: array[:, s * width : (s + 1) * width]

    def split_of(array, s):
        return lax.optimization_barrier(
            halves(jnp.where(row_ids < live[0, s], block_of(array, s), 0.0))
        )

    masks = (lax.broadcasted_iota(jnp.int32, (per_device, width), 1) < live.T).astype(jnp.float32)
    masks = lax.optimization_barrier(masks)

    def back_first(vecs, s):
        return jnp.dot(
            vecs * masks[s],
            block_of(tiles, s),
            precision=lax.Precision.HIGH,
            preferred_element_type=jnp.float32,
        )

    identity = jnp.eye(count, dtype=jnp.float32)
    own = lambda array: lax.dynamic_index_in_dim(cut(array, offs), off_index, 0, keepdims=False)

    def products(vecs, extra, back_of, block_for):
        near = permuted(vecs, lay.fetch)
        up = permuted(back_of(vecs, 1), lay.up)
        own_back = lax.optimization_barrier(back_of(vecs, 0))
        back = own_back + up
        returned = permuted(back, lay.back)
        far = permuted(near, lay.down)
        pair = gram(near, back)
        share = folded(pair + pair.T + gram(vecs, energies * vecs) * (1.0 / offs))
        block = block_for(0, own_back)
        first = lax.optimization_barrier(direct_product(near, block))
        block = block_for(1, block)
        second = lax.optimization_barrier(direct_product(far, block))
        share = row_total(jnp.concatenate([share] + extra, axis=0), lay)
        return first + second + returned, share

    def spread(chunk, share):
        got = sent_to_all(jnp.concatenate([chunk, share], axis=0), lay.row)
        return joined(got[:, :count]), unfolded(jnp.sum(got[:, count:], axis=0)) / total_rows

    chunk, precond_chunk, energy_chunk = own(vectors), own(precond[None]), own(energies[None])
    blocks = []

    def split_after(s, earlier):
        blocks.append(split_of(lax.optimization_barrier((tiles, earlier))[0], s))
        return blocks[s]

    part, share = products(vectors, [], back_first, split_after)
    image = jnp.sum(exchange(cut(part, offs), lay.row), axis=0)
    image = energy_chunk * chunk + image
    stepped, ritz = spread(chunk - precond_chunk * image, share)
    moved = stepped + precond * exact(ritz.T, vectors)

    moved_chunk = own(moved)
    part, share = products(
        moved,
        [folded(gram(moved, moved))],
        lambda vecs, s: back_product(vecs, blocks[s]),
        lambda s, _: blocks[s],
    )
    image = energy_chunk * moved_chunk + jnp.sum(exchange(cut(part, offs), lay.row), axis=0)
    fix = 1.5 * identity - 0.5 * unfolded(share[count // 2 :]) / total_rows
    chunk = exact(fix.T, moved_chunk - precond_chunk * image)
    stepped, ritz = spread(chunk, share[: count // 2])
    ritz = exact(exact(fix.T, ritz), fix)
    moved = stepped + precond * exact(ritz.T, exact(fix.T, moved))

    correlation = unfolded(line_total(folded(gram(moved, moved)), lay)) / total_rows
    return exact((1.5 * identity - 0.5 * correlation).T, moved), ritz


def solution(mesh):
    placed = (P(None, "row"), P("row", "off"), P("row", "off"), P("row"), P("row"))
    return jax.shard_map(
        local, mesh=mesh, in_specs=placed, out_specs=(P(None, "row"), P()), check_vma=False
    )
```

```python
import jax
import jax.numpy as jnp
from jax import lax
from jax.sharding import PartitionSpec as P


AXES = ("row", "off")


class Layout:
    def __init__(self, rows, offs, per_device):
        self.rows, self.offs, self.per = rows, offs, per_device
        number = lambda row, off: (row % rows) * offs + off
        every = [(row, p) for row in range(rows) for p in range(offs)]
        self.row = [[number(row, p) for p in range(offs)] for row in range(rows)]
        self.line = [
            [number(2 * chip + core, p) for chip in range(rows // 2)]
            for core in range(2)
            for p in range(offs)
        ]
        self.flip = {
            bit: [(number(row, p), number(row ^ bit, p)) for row, p in every]
            for bit in (1 << n for n in range(rows.bit_length() - 1))
        }
        turn = lambda row: row // 2 * 2 % offs
        self.fetch = [
            (number(row, p ^ turn(row)), number(row - per_device * p, p)) for row, p in every
        ]
        self.back = [(b, a) for a, b in self.fetch]
        self.up = [(number(row, p), number(row + 1, p)) for row, p in every]
        self.down = [(b, a) for a, b in self.up]


def exchange(array, groups):
    return lax.all_to_all(array, AXES, 0, 0, axis_index_groups=groups, tiled=True)


def sent_to_all(array, groups):
    peers = len(groups[0])
    return exchange(jnp.broadcast_to(array[None], (peers, *array.shape)), groups)


def exact(left, right):
    return jnp.dot(left, right, precision=lax.Precision.HIGHEST, preferred_element_type=jnp.float32)


def gram(left, right):
    return lax.dot_general(
        left,
        right,
        (((1,), (1,)), ((), ())),
        precision=lax.Precision.HIGHEST,
        preferred_element_type=jnp.float32,
    )


def cut(array, parts):
    k, width = array.shape
    return array.reshape(k, parts, width // parts).transpose(1, 0, 2)


def joined(array):
    parts, k, w = array.shape
    return array.transpose(1, 0, 2).reshape(k, parts * w)


def folded(square):
    half = square.shape[0] // 2
    return jnp.concatenate([square[:half], square[half:]], axis=1)


def unfolded(array):
    half = array.shape[0]
    return jnp.concatenate([array[:, : 2 * half], array[:, 2 * half :]], axis=0)


def permuted(array, pairs):
    return lax.ppermute(array, AXES, pairs)


def row_total(part, lay):
    for bit in sorted(lay.flip, reverse=True):
        part = part + permuted(part, lay.flip[bit])
    return part


def line_total(part, lay):
    part = part + permuted(part, lay.flip[1])
    return jnp.sum(sent_to_all(part, lay.line), axis=0)


def halves(array):
    high = lax.reduce_precision(array, 8, 7)
    return high.astype(jnp.bfloat16), (array - high).astype(jnp.bfloat16)


def block_product(vecs, block, dims):
    high, low = halves(vecs)
    count = vecs.shape[0]
    dot = lambda left, right: lax.dot_general(
        left, right, (dims, ((), ())), preferred_element_type=jnp.float32
    )
    main = dot(jnp.concatenate([high, low], axis=0), block[0])
    return main[:count] + (main[count:] + dot(high, block[1]))


def direct_product(piece, block):
    return block_product(piece, block, ((1,), (1,)))


def back_product(vecs, block):
    return block_product(vecs, block, ((1,), (0,)))


def local(vectors, tiles, live, energies, precond):
    count, width = vectors.shape
    per_device = tiles.shape[1] // width
    rows, offs = lax.axis_size("row"), lax.axis_size("off")
    lay = Layout(rows, offs, per_device)
    total_rows = width * rows
    part = width // offs
    off_index = lax.axis_index("off")
    row_ids = jnp.arange(width, dtype=jnp.int32)[:, None]
    block_of = lambda array, s: array[:, s * width : (s + 1) * width]

    def split_of(array, s):
        return lax.optimization_barrier(
            halves(jnp.where(row_ids < live[0, s], block_of(array, s), 0.0))
        )

    masks = (lax.broadcasted_iota(jnp.int32, (per_device, width), 1) < live.T).astype(jnp.float32)
    masks = lax.optimization_barrier(masks)

    def back_first(vecs, s):
        return jnp.dot(
            vecs * masks[s],
            block_of(tiles, s),
            precision=lax.Precision.HIGH,
            preferred_element_type=jnp.float32,
        )

    identity = jnp.eye(count, dtype=jnp.float32)
    own = lambda array: lax.dynamic_index_in_dim(cut(array, offs), off_index, 0, keepdims=False)

    def products(vecs, extra, back_of, block_for):
        near = permuted(vecs, lay.fetch)
        up = permuted(back_of(vecs, 1), lay.up)
        own_back = lax.optimization_barrier(back_of(vecs, 0))
        back = own_back + up
        returned = permuted(back, lay.back)
        far = permuted(near, lay.down)
        pair = gram(near, back)
        share = folded(pair + pair.T + gram(vecs, energies * vecs) * (1.0 / offs))
        block = block_for(0, own_back)
        first = lax.optimization_barrier(direct_product(near, block))
        block = block_for(1, block)
        second = lax.optimization_barrier(direct_product(far, block))
        share = row_total(jnp.concatenate([share] + extra, axis=0), lay)
        return first + second + returned, share

    def spread(chunk, share):
        got = sent_to_all(jnp.concatenate([chunk, share], axis=0), lay.row)
        return joined(got[:, :count]), unfolded(jnp.sum(got[:, count:], axis=0)) / total_rows

    chunk, precond_chunk, energy_chunk = own(vectors), own(precond[None]), own(energies[None])
    blocks = []

    def split_after(s, earlier):
        blocks.append(split_of(lax.optimization_barrier((tiles, earlier))[0], s))
        return blocks[s]

    part, share = products(vectors, [], back_first, split_after)
    image = jnp.sum(exchange(cut(part, offs), lay.row), axis=0)
    image = energy_chunk * chunk + image
    stepped, ritz = spread(chunk - precond_chunk * image, share)
    moved = stepped + precond * exact(ritz.T, vectors)

    moved_chunk = own(moved)
    part, share = products(
        moved,
        [folded(gram(moved, moved))],
        lambda vecs, s: back_product(vecs, blocks[s]),
        lambda s, _: blocks[s],
    )
    image = jnp.sum(exchange(cut(part, offs), lay.row), axis=0)
    image = energy_chunk * moved_chunk + image
    fix = 1.5 * identity - 0.5 * unfolded(share[count // 2 :]) / total_rows
    chunk = exact(fix.T, moved_chunk - precond_chunk * image)
    stepped, ritz = spread(chunk, share[: count // 2])
    ritz = exact(exact(fix.T, ritz), fix)
    moved = stepped + precond * exact(ritz.T, exact(fix.T, moved))

    correlation = unfolded(line_total(folded(gram(moved, moved)), lay)) / total_rows
    return exact((1.5 * identity - 0.5 * correlation).T, moved), ritz


def solution(mesh):
    placed = (P(None, "row"), P("row", "off"), P("row", "off"), P("row"), P("row"))
    return jax.shard_map(
        local, mesh=mesh, in_specs=placed, out_specs=(P(None, "row"), P()), check_vma=False
    )
```

```python
import jax
import jax.numpy as jnp
from jax import lax
from jax.sharding import PartitionSpec as P


AXES = ("row", "off")


class Layout:
    def __init__(self, rows, offs, per_device):
        self.rows, self.offs, self.per = rows, offs, per_device
        number = lambda row, off: (row % rows) * offs + off
        every = [(row, p) for row in range(rows) for p in range(offs)]
        self.row = [[number(row, p) for p in range(offs)] for row in range(rows)]
        self.line = [
            [number(2 * chip + core, p) for chip in range(rows // 2)]
            for core in range(2)
            for p in range(offs)
        ]
        self.flip = {
            bit: [(number(row, p), number(row ^ bit, p)) for row, p in every]
            for bit in (1 << n for n in range(rows.bit_length() - 1))
        }
        cycle = (2, 0, 6, 4)
        sender = {
            (chip, cycle[(q // 2 + chip) % 4] + q % 2): q for chip in range(rows // 2) for q in range(8)
        }
        self.fetch = []
        for row, p in every:
            far = (row + per_device * p) % rows
            self.fetch.append((number(far, sender[far // 2, p]), number(row, p)))
        self.back = [(b, a) for a, b in self.fetch]
        self.up = [(number(row, p), number(row + 1, p)) for row, p in every]
        self.down = [(b, a) for a, b in self.up]


def exchange(array, groups):
    return lax.all_to_all(array, AXES, 0, 0, axis_index_groups=groups, tiled=True)


def sent_to_all(array, groups):
    peers = len(groups[0])
    return exchange(jnp.broadcast_to(array[None], (peers, *array.shape)), groups)


def exact(left, right):
    return jnp.dot(left, right, precision=lax.Precision.HIGHEST, preferred_element_type=jnp.float32)


def gram(left, right):
    return lax.dot_general(
        left,
        right,
        (((1,), (1,)), ((), ())),
        precision=lax.Precision.HIGHEST,
        preferred_element_type=jnp.float32,
    )


def cut(array, parts):
    k, width = array.shape
    return array.reshape(k, parts, width // parts).transpose(1, 0, 2)


def joined(array):
    parts, k, w = array.shape
    return array.transpose(1, 0, 2).reshape(k, parts * w)


def folded(square):
    half = square.shape[0] // 2
    return jnp.concatenate([square[:half], square[half:]], axis=1)


def unfolded(array):
    half = array.shape[0]
    return jnp.concatenate([array[:, : 2 * half], array[:, 2 * half :]], axis=0)


def permuted(array, pairs):
    return lax.ppermute(array, AXES, pairs)


def row_total(part, lay):
    for bit in sorted(lay.flip, reverse=True):
        part = part + permuted(part, lay.flip[bit])
    return part


def line_total(part, lay):
    part = jnp.sum(sent_to_all(part, lay.line), axis=0)
    return part + permuted(part, lay.flip[1])


def halves(array):
    high = lax.reduce_precision(array, 8, 7)
    return high.astype(jnp.bfloat16), (array - high).astype(jnp.bfloat16)


def block_product(vecs, block, dims):
    high, low = halves(vecs)
    count = vecs.shape[0]
    dot = lambda left, right: lax.dot_general(
        left, right, (dims, ((), ())), preferred_element_type=jnp.float32
    )
    main = dot(jnp.concatenate([high, low], axis=0), block[0])
    return main[:count] + (main[count:] + dot(high, block[1]))


def direct_product(piece, block):
    return block_product(piece, block, ((1,), (1,)))


def back_product(vecs, block):
    return block_product(vecs, block, ((1,), (0,)))


def local(vectors, tiles, live, energies, precond):
    count, width = vectors.shape
    per_device = tiles.shape[1] // width
    rows, offs = lax.axis_size("row"), lax.axis_size("off")
    lay = Layout(rows, offs, per_device)
    total_rows = width * rows
    part = width // offs
    off_index = lax.axis_index("off")
    row_ids = jnp.arange(width, dtype=jnp.int32)[:, None]
    block_of = lambda array, s: array[:, s * width : (s + 1) * width]

    def split_of(array, s):
        return lax.optimization_barrier(
            halves(jnp.where(row_ids < live[0, s], block_of(array, s), 0.0))
        )

    masks = (lax.broadcasted_iota(jnp.int32, (per_device, width), 1) < live.T).astype(jnp.float32)
    masks = lax.optimization_barrier(masks)

    def back_first(vecs, s):
        return jnp.dot(
            vecs * masks[s],
            block_of(tiles, s),
            precision=lax.Precision.HIGH,
            preferred_element_type=jnp.float32,
        )

    identity = jnp.eye(count, dtype=jnp.float32)
    own = lambda array: lax.dynamic_index_in_dim(cut(array, offs), off_index, 0, keepdims=False)

    def products(vecs, extra, back_of, block_for):
        near = permuted(vecs, lay.fetch)
        up = permuted(back_of(vecs, 1), lay.up)
        own_back = lax.optimization_barrier(back_of(vecs, 0))
        back = own_back + up
        returned = permuted(back, lay.back)
        far = permuted(near, lay.down)
        pair = gram(near, back)
        share = folded(pair + pair.T + gram(vecs, energies * vecs) * (1.0 / offs))
        block = block_for(0, own_back)
        first = lax.optimization_barrier(direct_product(near, block))
        block = block_for(1, block)
        second = lax.optimization_barrier(direct_product(far, block))
        share = row_total(jnp.concatenate([share] + extra, axis=0), lay)
        return first + second + returned, share

    def spread(chunk, share):
        got = sent_to_all(jnp.concatenate([chunk, share], axis=0), lay.row)
        return joined(got[:, :count]), unfolded(jnp.sum(got[:, count:], axis=0)) / total_rows

    chunk, precond_chunk, energy_chunk = own(vectors), own(precond[None]), own(energies[None])
    blocks = []

    def split_after(s, earlier):
        blocks.append(split_of(lax.optimization_barrier((tiles, earlier))[0], s))
        return blocks[s]

    part, share = products(vectors, [], back_first, split_after)
    image = jnp.sum(exchange(cut(part, offs), lay.row), axis=0)
    image = energy_chunk * chunk + image
    stepped, ritz = spread(chunk - precond_chunk * image, share)
    moved = stepped + precond * exact(ritz.T, vectors)

    moved_chunk = own(moved)
    part, share = products(
        moved,
        [folded(gram(moved, moved))],
        lambda vecs, s: back_product(vecs, blocks[s]),
        lambda s, _: blocks[s],
    )
    image = energy_chunk * moved_chunk + jnp.sum(exchange(cut(part, offs), lay.row), axis=0)
    fix = 1.5 * identity - 0.5 * unfolded(share[count // 2 :]) / total_rows
    chunk = exact(fix.T, moved_chunk - precond_chunk * image)
    stepped, ritz = spread(chunk, share[: count // 2])
    ritz = exact(exact(fix.T, ritz), fix)
    moved = stepped + precond * exact(ritz.T, exact(fix.T, moved))

    correlation = unfolded(line_total(folded(gram(moved, moved)), lay)) / total_rows
    return exact((1.5 * identity - 0.5 * correlation).T, moved), ritz


def solution(mesh):
    placed = (P(None, "row"), P("row", "off"), P("row", "off"), P("row"), P("row"))
    return jax.shard_map(
        local, mesh=mesh, in_specs=placed, out_specs=(P(None, "row"), P()), check_vma=False
    )
```

```python
import jax
import jax.numpy as jnp
from jax import lax
from jax.sharding import PartitionSpec as P


AXES = ("row", "off")


class Layout:
    def __init__(self, rows, offs, per_device):
        self.rows, self.offs, self.per = rows, offs, per_device
        number = lambda row, off: (row % rows) * offs + off
        every = [(row, p) for row in range(rows) for p in range(offs)]
        self.row = [[number(row, p) for p in range(offs)] for row in range(rows)]
        self.line = [
            [number(2 * chip + core, p) for chip in range(rows // 2)]
            for core in range(2)
            for p in range(offs)
        ]
        self.flip = {
            bit: [(number(row, p), number(row ^ bit, p)) for row, p in every]
            for bit in (1 << n for n in range(rows.bit_length() - 1))
        }
        turn = lambda row: row // 2 * 2 % offs
        self.fetch = [
            (number(row, p ^ turn(row)), number(row - per_device * p, p)) for row, p in every
        ]
        self.back = [(b, a) for a, b in self.fetch]
        self.up = [(number(row, p), number(row + 1, p)) for row, p in every]
        self.down = [(b, a) for a, b in self.up]


def exchange(array, groups):
    return lax.all_to_all(array, AXES, 0, 0, axis_index_groups=groups, tiled=True)


def sent_to_all(array, groups):
    peers = len(groups[0])
    return exchange(jnp.broadcast_to(array[None], (peers, *array.shape)), groups)


def exact(left, right):
    return jnp.dot(left, right, precision=lax.Precision.HIGHEST, preferred_element_type=jnp.float32)


def gram(left, right):
    return lax.dot_general(
        left,
        right,
        (((1,), (1,)), ((), ())),
        precision=lax.Precision.HIGHEST,
        preferred_element_type=jnp.float32,
    )


def cut(array, parts):
    k, width = array.shape
    return array.reshape(k, parts, width // parts).transpose(1, 0, 2)


def joined(array):
    parts, k, w = array.shape
    return array.transpose(1, 0, 2).reshape(k, parts * w)


def folded(square):
    half = square.shape[0] // 2
    return jnp.concatenate([square[:half], square[half:]], axis=1)


def unfolded(array):
    half = array.shape[0]
    return jnp.concatenate([array[:, : 2 * half], array[:, 2 * half :]], axis=0)


def permuted(array, pairs):
    return lax.ppermute(array, AXES, pairs)


def row_total(part, lay):
    for bit in sorted(lay.flip, reverse=True):
        part = part + permuted(part, lay.flip[bit])
    return part


def line_total(part, lay):
    part = jnp.sum(sent_to_all(part, lay.line), axis=0)
    return part + permuted(part, lay.flip[1])


def direct_product(piece, block, mask):
    term = lax.dot_general(
        piece,
        block,
        (((1,), (1,)), ((), ())),
        precision=lax.Precision.HIGH,
        preferred_element_type=jnp.float32,
    )
    return mask * term


def back_product(vectors, block, mask):
    return jnp.dot(
        vectors * mask, block, precision=lax.Precision.HIGH, preferred_element_type=jnp.float32
    )


def local(vectors, tiles, live, energies, precond):
    count, width = vectors.shape
    per_device = tiles.shape[1] // width
    rows, offs = lax.axis_size("row"), lax.axis_size("off")
    lay = Layout(rows, offs, per_device)
    total_rows = width * rows
    part = width // offs
    off_index = lax.axis_index("off")
    row_ids = jnp.arange(width, dtype=jnp.int32)
    masks = (lax.broadcasted_iota(jnp.int32, (per_device, width), 1) < live.T).astype(jnp.float32)
    masks = lax.optimization_barrier(masks)
    blocks = [tiles[:, s * width : (s + 1) * width] for s in range(per_device)]
    identity = jnp.eye(count, dtype=jnp.float32)
    own = lambda array: lax.dynamic_index_in_dim(cut(array, offs), off_index, 0, keepdims=False)

    def products(vecs, extra):
        near = permuted(vecs, lay.fetch)
        up = permuted(back_product(vecs, blocks[1], masks[1]), lay.up)
        back = back_product(vecs, blocks[0], masks[0])
        back = lax.optimization_barrier(back) + up
        returned = permuted(back, lay.back)
        far = permuted(near, lay.down)
        pair = gram(near, back)
        share = folded(pair + pair.T + gram(vecs, energies * vecs) * (1.0 / offs))
        first = direct_product(near, blocks[0], masks[0])
        second = direct_product(far, blocks[1], masks[1])
        first, second = lax.optimization_barrier(first), lax.optimization_barrier(second)
        share = row_total(jnp.concatenate([share] + extra, axis=0), lay)
        return first + second + returned, share

    def spread(chunk, share):
        got = sent_to_all(jnp.concatenate([chunk, share], axis=0), lay.row)
        return joined(got[:, :count]), unfolded(jnp.sum(got[:, count:], axis=0)) / total_rows

    chunk, precond_chunk, energy_chunk = own(vectors), own(precond[None]), own(energies[None])
    part, share = products(vectors, [])
    image = jnp.sum(exchange(cut(part, offs), lay.row), axis=0)
    image = energy_chunk * chunk + image
    stepped, ritz = spread(chunk - precond_chunk * image, share)
    moved = stepped + precond * exact(ritz.T, vectors)

    moved_chunk = own(moved)
    part, share = products(moved, [folded(gram(moved, moved))])
    image = jnp.sum(exchange(cut(part, offs), lay.row), axis=0)
    image = energy_chunk * moved_chunk + image
    fix = 1.5 * identity - 0.5 * unfolded(share[count // 2 :]) / total_rows
    chunk = exact(fix.T, moved_chunk - precond_chunk * image)
    stepped, ritz = spread(chunk, share[: count // 2])
    ritz = exact(exact(fix.T, ritz), fix)
    moved = stepped + precond * exact(ritz.T, exact(fix.T, moved))

    correlation = unfolded(line_total(folded(gram(moved, moved)), lay)) / total_rows
    return exact((1.5 * identity - 0.5 * correlation).T, moved), ritz


def solution(mesh):
    placed = (P(None, "row"), P("row", "off"), P("row", "off"), P("row"), P("row"))
    return jax.shard_map(
        local, mesh=mesh, in_specs=placed, out_specs=(P(None, "row"), P()), check_vma=False
    )
```
